32 devices in a mesh: groups: 2 (over y), ctx: 4 (over z), head: 4 (over x, core).
Axes of the slice: x: 2, y: 2, z: 4, core: 2. Of those that a mesh axis runs over, the one named last changes fastest.
Arguments:
- query_rows: bfloat16 [3072, 3072], P(('groups', 'ctx', 'head')), parts along dimension 0, may hold values from -150 to 150
- key_rows: bfloat16 [3072, 3072], P(('groups', 'ctx', 'head')), parts along dimension 0, may hold values from -6 to 6
- value_rows: bfloat16 [3072, 3072], P(('groups', 'ctx', 'head')), parts along dimension 0, may hold values from -6 to 6
- tile_mask: int32 [8, 27], P(('groups', 'ctx')), parts along dimension 0, may hold values from 0 to 1, as said below
Outputs:
- attended: bfloat16 [3072, 3072], P(('groups', 'ctx', 'head')), parts along dimension 0
The draws below stay inside these ranges and needn't reach their ends.
There are 2 independent parts, one for each index of `groups`. The reference program is written for one: setup_inputs(seed, part) draws one part's arguments, and reference() takes and returns one part's arrays. A program takes and returns all parts, laid end to end along the dimension named above; each array names one. Nothing has to cross between parts.
Inputs may be any that keep to these rules, and one draw needn't show every extreme that they name: `tile_mask`: entry o of row i is 1 only where the key tile of offset o lies inside the grid; entry 13 is always 1; a row has at most 4 ones, and some row has exactly 4.
All inputs are finite; a program needn't handle non-finite values.
Results may differ from the reference program's by a relative error of at most 0.0023.
Values may be sent and summed in bfloat16 or wider, within the bound.
No kernel may reach another device: no remote copies, remote signals or barrier semaphores. Data moves between devices by JAX's collectives and lax.ppermute only.
A program may use at most 64 MiB of HBM per device.

```python
import math
import jax
import jax.numpy as jnp
from jax import lax

HEADS = 24
HDIM = 128
D = 3072
TILE = 384
NTT = 1
DH = 2
DW = 2
KEPT = 4
TOKENS = 1536


def paired_fields(key):
    folded = jax.random.fold_in(key, 7)
    draw_keys = jax.random.split(folded, 3)
    queries = jnp.clip(jax.random.normal(draw_keys[0], (TOKENS, HEADS * HDIM), jnp.float32), -6.0, 6.0)
    key_field = jnp.clip(jax.random.normal(draw_keys[1], (TOKENS, HEADS * HDIM), jnp.float32), -6.0, 6.0)
    spread = jnp.exp(jax.random.uniform(draw_keys[2], (TOKENS, HEADS, 1), jnp.float32, 0.0, math.log(8.0)))
    queries = (queries.reshape(TOKENS, HEADS, HDIM) * spread).reshape(TOKENS, HEADS * HDIM)
    return (queries, key_field)


def draw_query_rows(key, part):
    return paired_fields(key)[0].astype(jnp.bfloat16)


def draw_key_rows(key, part):
    return paired_fields(key)[1].astype(jnp.bfloat16)


def draw_tile_mask(key, part):
    folded = jax.random.fold_in(key, 11)
    draw_keys = jax.random.split(folded, 2)
    tile_count = DH * DW * NTT
    block_total = DH * DW
    rotation = DW // 2
    tile_index = jnp.arange(tile_count, dtype=jnp.int32)
    frame_pos = tile_index % NTT
    grid_pos = (tile_index // NTT - rotation) % block_total
    column = grid_pos % DW
    grid_row = grid_pos // DW
    offset = jnp.arange(27, dtype=jnp.int32)
    step_frame = offset // 9 - 1
    step_row = offset // 3 % 3 - 1
    step_col = offset % 3 - 1
    frame_to = frame_pos[:, None] + step_frame[None, :]
    row_to = grid_row[:, None] + step_row[None, :]
    col_to = column[:, None] + step_col[None, :]
    inside = (frame_to >= 0) & (frame_to < NTT) & (row_to >= 0) & (row_to < DH) & (col_to >= 0) & (col_to < DW)
    counts = jax.random.randint(draw_keys[0], (tile_count,), 1, KEPT + 1, jnp.int32)
    forced_pos = min(1, DH - 1) * DW + min(1, DW - 1)
    forced = (forced_pos + rotation) % block_total * NTT + min(1, NTT - 1)
    counts = jnp.where(tile_index == forced, KEPT, counts)
    priority_noise = jax.random.randint(draw_keys[1], (tile_count, 27), 0, 1 << 20, jnp.int32) * 32 + offset[None, :]
    priority = jnp.where(offset[None, :] == 13, -1, jnp.where(inside, priority_noise, (1 << 26) + offset[None, :]))
    ranking = jnp.argsort(jnp.argsort(priority, axis=1), axis=1)
    return ((ranking < counts[:, None]) & inside).astype(jnp.int32)


def level_of(stream_key, shape, shards, least, high):
    def one(dim, blocks):
        steps = jax.random.uniform(jax.random.fold_in(jax.random.fold_in(stream_key, 6), dim), (blocks,), jnp.float32, least / len(shards), high / len(shards))
        return jnp.repeat(jnp.exp(steps), shape[dim] // blocks).reshape((-1,) + (1,) * (len(shape) - dim - 1))

    level = one(*shards[0])
    for cut in shards[1:]:
        level = level * one(*cut)
    return level


def gaussian(own_key, shape, deviation, most, cuts=(), kind=jnp.bfloat16):
    factor_of = level_of(own_key, shape, cuts, -0.22, 0.18) if cuts else 1.0
    entries = jax.random.normal(own_key, shape, jnp.float32) * deviation * factor_of
    return jnp.minimum(jnp.maximum(entries, -most), most).astype(kind)


def setup_inputs(seed: int = 0, part: int = 0) -> dict:
    keys = jax.random.split(jax.random.key(seed), 5)
    part_keys = jax.random.split(jax.random.fold_in(keys[4], part), 5)
    query_rows = draw_query_rows(jax.random.fold_in(jax.random.fold_in(keys[4], part), 71), part)
    key_rows = draw_key_rows(jax.random.fold_in(jax.random.fold_in(keys[4], part), 71), part)
    value_rows = gaussian(part_keys[2], (TOKENS, D), 1.0, 6.0, ((0, 16),))
    tile_mask = draw_tile_mask(jax.random.fold_in(jax.random.fold_in(keys[4], part), 71), part)
    return {"query_rows": query_rows, "key_rows": key_rows, "value_rows": value_rows, "tile_mask": tile_mask}


def reference(query_rows, key_rows, value_rows, tile_mask):
    block_total = DH * DW
    rotation = DW // 2
    flat_shape = (block_total, NTT, TILE, HEADS, HDIM)
    grid_shape = (DH, DW, NTT, TILE, HEADS, HDIM)
    query_grid = jnp.roll(query_rows.reshape(flat_shape), -rotation, axis=0).reshape(grid_shape)
    key_grid = jnp.roll(key_rows.reshape(flat_shape), -rotation, axis=0).reshape(grid_shape)
    value_grid = jnp.roll(value_rows.reshape(flat_shape), -rotation, axis=0).reshape(grid_shape)
    padding = ((1, 1), (1, 1), (1, 1), (0, 0), (0, 0), (0, 0))
    key_padded = jnp.pad(key_grid, padding)
    value_padded = jnp.pad(value_grid, padding)
    mask_grid = jnp.roll(tile_mask.reshape(block_total, NTT, 27), -rotation, axis=0).reshape(DH, DW, NTT, 27)
    score_scale = 1.0 / math.sqrt(HDIM)
    zero_index = jnp.zeros((), jnp.int32)
    frame_steps = [0, 1, 2] if NTT > 1 else [1]
    first_col = 9 * frame_steps[0]
    col_count = 9 * len(frame_steps)

    def one_block(block_index):
        block_row = (block_index // DW).astype(jnp.int32)
        block_col = (block_index % DW).astype(jnp.int32)
        start = (block_row, block_col, zero_index, zero_index, zero_index, zero_index)
        extent = (3, 3, NTT + 2, TILE, HEADS, HDIM)
        key_window = lax.dynamic_slice(key_padded, start, extent)
        value_window = lax.dynamic_slice(value_padded, start, extent)
        query_block = lax.dynamic_slice(query_grid, start, (1, 1, NTT, TILE, HEADS, HDIM)).reshape(NTT, TILE, HEADS, HDIM)
        mask_rows = lax.dynamic_slice(mask_grid, (block_row, block_col, zero_index, zero_index), (1, 1, NTT, 27)).reshape(NTT, 27)
        mask_rows = mask_rows[:, first_col:first_col + col_count]
        key_stack = jnp.stack([key_window[:, :, shift_frame:shift_frame + NTT] for shift_frame in frame_steps])
        key_stack = jnp.moveaxis(key_stack, 3, 0).reshape(NTT, col_count * TILE, HEADS, HDIM)
        value_stack = jnp.stack([value_window[:, :, shift_frame:shift_frame + NTT] for shift_frame in frame_steps])
        value_stack = jnp.moveaxis(value_stack, 3, 0).reshape(NTT, col_count * TILE, HEADS, HDIM)
        scores = jnp.einsum('fqhd,fkhd->fhqk', query_block.astype(jnp.float32), key_stack.astype(jnp.float32)) * score_scale
        kept_mask = jnp.repeat(mask_rows == 1, TILE, axis=1)[:, None, None, :]
        row_peak = lax.optimization_barrier(jnp.max(jnp.where(kept_mask, scores, -jnp.inf), axis=3, keepdims=True))
        weight = jnp.exp(jnp.where(kept_mask, scores - row_peak, -jnp.inf))
        row_total = lax.optimization_barrier(jnp.sum(weight, axis=3, keepdims=True))
        rounded = lax.optimization_barrier(weight.astype(jnp.bfloat16)).astype(jnp.float32)
        mixed_heads = jnp.einsum('fhqk,fkhd->fhqd', rounded, value_stack.astype(jnp.float32)) / row_total
        return jnp.transpose(mixed_heads, (0, 2, 1, 3)).astype(jnp.bfloat16)
    blocks = lax.map(one_block, jnp.arange(block_total, dtype=jnp.int32))
    blocks = jnp.roll(blocks.reshape(block_total, NTT, TILE, HEADS, HDIM), rotation, axis=0)
    return blocks.reshape(TOKENS, HEADS * HDIM)
```

```python
import functools
import math

import jax
import jax.numpy as jnp
from jax import lax
from jax.experimental import pallas as pl
from jax.experimental.pallas import tpu as pltpu
from jax.sharding import Mesh, PartitionSpec as P

HDIM = 128


def passed_along(block, axis, distance):
    devices = range(lax.axis_size(axis))
    route = [((i - distance) % len(devices), i) for i in devices]
    return lax.ppermute(block, axis, route)


def on_device(query_rows, key_rows, value_rows, tile_mask):
    cycle_size = lax.axis_size("ctx")
    grid_rows = max(2, cycle_size // 8)
    grid_cols = cycle_size // grid_rows
    query_local, key_local, value_local = (
        lax.all_to_all(query_rows, "head", split_axis=1, concat_axis=0, tiled=True),
        lax.all_to_all(key_rows, "head", split_axis=1, concat_axis=0, tiled=True),
        lax.all_to_all(value_rows, "head", split_axis=1, concat_axis=0, tiled=True),
    )
    feature_width = query_local.shape[1]
    head_count = feature_width // HDIM
    frames = tile_mask.shape[0]
    tile_len = query_local.shape[0] // frames
    key_value = jnp.stack([key_local, value_local]).reshape(2, frames, tile_len, feature_width)
    row_parts = [passed_along(key_value, "ctx", shift_by) for shift_by in (1, -1)]
    row_strip = jnp.stack([row_parts[0], key_value, row_parts[1]])
    column_parts = [
        passed_along(row_strip, "ctx", shift_by) for shift_by in (grid_cols, -grid_cols)
    ]
    window = jnp.stack([column_parts[0], row_strip, column_parts[1]])
    key_tiles = window[:, :, 0].reshape(9 * frames, tile_len, feature_width)
    value_tiles = window[:, :, 1].reshape(9 * frames, tile_len, feature_width)
    kept_mask = tile_mask == 1
    first_offset = 9
    slot_count = 9
    slot_order = jnp.arange(first_offset, first_offset + slot_count, dtype=jnp.int32)[None, :]
    slot_kept = kept_mask[:, first_offset : first_offset + slot_count]
    frame_ids = jnp.arange(frames, dtype=jnp.int32)[:, None]
    source_frame = jnp.clip(frame_ids + slot_order // 9 - 1, 0, frames - 1)
    source = slot_order % 9 * frames + source_frame
    kept_cols = jnp.repeat(slot_kept, tile_len, axis=1)[:, None, :]
    score_scale = 1.0 / math.sqrt(HDIM)

    def one_head(head_index):
        column_start = head_index * HDIM
        key_head = lax.dynamic_slice_in_dim(key_tiles, column_start, HDIM, 2)
        value_head = lax.dynamic_slice_in_dim(value_tiles, column_start, HDIM, 2)
        query_head = lax.dynamic_slice_in_dim(query_local, column_start, HDIM, 1).reshape(
            frames, tile_len, HDIM
        )
        picked_keys = jnp.take(key_head, source, axis=0).reshape(
            frames, slot_count * tile_len, HDIM
        )
        picked_values = jnp.take(value_head, source, axis=0).reshape(
            frames, slot_count * tile_len, HDIM
        )
        scores = (
            jnp.einsum("fqd,fkd->fqk", query_head, picked_keys, preferred_element_type=jnp.float32)
            * score_scale
        )
        row_peak = jnp.max(jnp.where(kept_cols, scores, -jnp.inf), axis=2, keepdims=True)
        weight = jnp.exp(jnp.where(kept_cols, scores - row_peak, -jnp.inf))
        row_total = jnp.sum(weight, axis=2, keepdims=True)
        rounded = weight.astype(jnp.bfloat16)
        mixed = jnp.einsum(
            "fqk,fkd->fqd", rounded, picked_values, preferred_element_type=jnp.float32
        )
        return (mixed / row_total).astype(jnp.bfloat16)

    result = lax.map(one_head, jnp.arange(head_count, dtype=jnp.int32))
    result = jnp.transpose(result, (1, 2, 0, 3)).reshape(frames * tile_len, feature_width)
    return lax.all_to_all(result, "head", split_axis=0, concat_axis=1, tiled=True)


def flipped(index, bits, size):
    out, step = 0, 1
    while step < size:
        bit = (index // step) % 2
        out = out + step * (1 - bit if (bits // step) % 2 else bit)
        step *= 2
    return out


def group_of(s, heads):
    mate = flipped(lax.axis_index("mate"), (s // heads) % 2, 2)
    return mate * heads + flipped(lax.axis_index("head"), s % heads, heads)


def cut_kernel(heads, width, q_ref, k_ref, v_ref, *rest):
    outs, sem = rest[:-1], rest[-1]
    copies = []
    for s, out in enumerate(outs):
        cols = pl.ds(pl.multiple_of(group_of(s, heads) * width, 128), width)
        parts = (q_ref, k_ref, v_ref) if s < 2 * heads else (k_ref, v_ref)
        for n, part in enumerate(parts):
            copies.append(
                pltpu.make_async_copy(
                    part.at[:, cols], out.at[:, n * width : (n + 1) * width], sem.at[len(copies)]
                )
            )
    for copy in copies:
        copy.start()
    for copy in copies:
        copy.wait()


def cut(query_rows, key_rows, value_rows, heads, width):
    rows = query_rows.shape[0]
    near, far = 2 * heads, 2 * heads
    shapes = [jax.ShapeDtypeStruct((rows, 3 * width), jnp.bfloat16)] * near + [
        jax.ShapeDtypeStruct((rows, 2 * width), jnp.bfloat16)
    ] * far
    return pl.pallas_call(
        functools.partial(cut_kernel, heads, width),
        out_shape=shapes,
        in_specs=[pl.BlockSpec(memory_space=pltpu.VMEM)] * 3,
        out_specs=[pl.BlockSpec(memory_space=pl.ANY)] * (near + far),
        scratch_shapes=[pltpu.SemaphoreType.DMA((3 * near + 2 * far,))],
        name="cut",
    )(query_rows, key_rows, value_rows)


def attend_kernel(heads, width, *refs):
    count = 4 * heads
    masks = refs[:2]
    pieces = refs[2 : 2 + count]
    outs = refs[2 + count : 2 + count + 2 * heads]
    qbuf, kbuf, vbuf = refs[2 + count + 2 * heads :]
    rows = pieces[0].shape[0]
    tile = heads * rows
    z = lax.axis_index("pair") * 2 + lax.axis_index("mate")
    for s, piece in enumerate(pieces):
        at = pl.ds(s * rows, rows)
        base = 0
        if s < 2 * heads:
            qbuf[at, :] = piece[:, :width]
            base = width
        kbuf[at, :] = piece[:, base : base + width]
        vbuf[at, :] = piece[:, base + width : base + 2 * width]
    lane_tile = lax.broadcasted_iota(jnp.int32, (1, 4 * tile), 1) // tile

    def place(block):
        p = (block + 3) % 4
        return p // 2, p % 2

    factor = math.log2(math.e) / math.sqrt(HDIM)
    for own in range(2):
        row, col = place(flipped(z, own, 4))
        bias = jnp.zeros((1, 4 * tile), jnp.float32)
        for kt in range(4):
            key_row, key_col = place(flipped(z, kt, 4))
            offset = 9 + 3 * (key_row - row + 1) + (key_col - col + 1)
            kept = masks[own][0, offset] == 1
            bias = jnp.where((lane_tile == kt) & jnp.logical_not(kept), -jnp.inf, bias)

        def one_head(h, carry):
            cols = pl.ds(pl.multiple_of(h * HDIM, HDIM), HDIM)
            q = qbuf[own * tile : (own + 1) * tile, cols]
            scores = lax.dot_general(
                q, kbuf[:, cols], (((1,), (1,)), ((), ())), preferred_element_type=jnp.float32
            )
            scores = scores + bias
            peak = jnp.max(scores, axis=1, keepdims=True)
            weight = jnp.exp2((scores - peak) * factor)
            total = jnp.sum(weight, axis=1, keepdims=True)
            mixed = jnp.dot(
                weight.astype(jnp.bfloat16), vbuf[:, cols], preferred_element_type=jnp.float32
            )
            result = (mixed / total).astype(jnp.bfloat16)
            for n in range(heads):
                outs[own * heads + n][:, cols] = result[n * rows : (n + 1) * rows]
            return carry

        lax.fori_loop(0, width // HDIM, one_head, 0)


def attend(masks, pieces, heads, width):
    rows = pieces[0].shape[0]
    tile = heads * rows
    vmem = pl.BlockSpec(memory_space=pltpu.VMEM)
    return pl.pallas_call(
        functools.partial(attend_kernel, heads, width),
        out_shape=[jax.ShapeDtypeStruct((rows, width), jnp.bfloat16)] * (2 * heads),
        in_specs=[pl.BlockSpec(memory_space=pltpu.SMEM)] * 2 + [vmem] * len(pieces),
        out_specs=[vmem] * (2 * heads),
        scratch_shapes=[
            pltpu.VMEM((2 * tile, width), jnp.bfloat16),
            pltpu.VMEM((4 * tile, width), jnp.bfloat16),
            pltpu.VMEM((4 * tile, width), jnp.bfloat16),
        ],
        name="attend",
    )(*masks, *pieces)


def join_kernel(heads, width, *refs):
    pieces, out = refs[:-1], refs[-1]
    for s, piece in enumerate(pieces):
        cols = pl.ds(pl.multiple_of(group_of(s, heads) * width, 128), width)
        out[:, cols] = piece[...]


def join(pieces, heads, width):
    rows = pieces[0].shape[0]
    vmem = pl.BlockSpec(memory_space=pltpu.VMEM)
    return pl.pallas_call(
        functools.partial(join_kernel, heads, width),
        out_shape=jax.ShapeDtypeStruct((rows, 2 * heads * width), jnp.bfloat16),
        in_specs=[vmem] * len(pieces),
        out_specs=vmem,
        name="join",
    )(*pieces)


AXES = ("pair", "mate", "head")


def exchanged(block, s, heads):
    return lax.ppermute(block, AXES, [(i, i ^ s) for i in range(4 * heads)])


def on_device_square(query_rows, key_rows, value_rows, tile_mask):
    heads = lax.axis_size("head")
    width = query_rows.shape[1] // (2 * heads)
    sent = cut(query_rows, key_rows, value_rows, heads, width)
    pieces = [sent[0]] + [exchanged(sent[s], s, heads) for s in range(1, 4 * heads)]
    masks = (tile_mask, exchanged(tile_mask, heads, heads))
    parts = attend(masks, pieces, heads, width)
    back = [parts[0]] + [exchanged(parts[s], s, heads) for s in range(1, 2 * heads)]
    return join(back, heads, width)


def solution(mesh):
    groups, ctx, heads = (mesh.shape[name] for name in ("groups", "ctx", "head"))
    if ctx == 4 and heads & (heads - 1) == 0:
        square = Mesh(mesh.devices.reshape(groups, 2, 2, heads), ("groups",) + AXES)
        rows = P(("groups",) + AXES, None)
        return jax.shard_map(
            on_device_square,
            mesh=square,
            in_specs=(rows, rows, rows, P(("groups", "pair", "mate"), None)),
            out_specs=rows,
            check_vma=False,
        )
    rows = P(("groups", "ctx", "head"), None)
    return jax.shard_map(
        on_device,
        mesh=mesh,
        in_specs=(rows, rows, rows, P(("groups", "ctx"), None)),
        out_specs=rows,
        check_vma=False,
    )
```

```python
import functools
import math

import jax
import jax.numpy as jnp
from jax import lax
from jax.experimental import pallas as pl
from jax.experimental.pallas import tpu as pltpu
from jax.sharding import Mesh, PartitionSpec as P


HDIM = 128


def passed_along(block, axis, distance):
    devices = range(lax.axis_size(axis))
    route = [((i - distance) % len(devices), i) for i in devices]
    return lax.ppermute(block, axis, route)


def on_device(query_rows, key_rows, value_rows, tile_mask):
    cycle_size = lax.axis_size("ctx")
    grid_rows = max(2, cycle_size // 8)
    grid_cols = cycle_size // grid_rows
    query_local, key_local, value_local = (
        lax.all_to_all(query_rows, "head", split_axis=1, concat_axis=0, tiled=True),
        lax.all_to_all(key_rows, "head", split_axis=1, concat_axis=0, tiled=True),
        lax.all_to_all(value_rows, "head", split_axis=1, concat_axis=0, tiled=True),
    )
    feature_width = query_local.shape[1]
    head_count = feature_width // HDIM
    frames = tile_mask.shape[0]
    tile_len = query_local.shape[0] // frames
    key_value = jnp.stack([key_local, value_local]).reshape(2, frames, tile_len, feature_width)
    row_parts = [passed_along(key_value, "ctx", shift_by) for shift_by in (1, -1)]
    row_strip = jnp.stack([row_parts[0], key_value, row_parts[1]])
    column_parts = [
        passed_along(row_strip, "ctx", shift_by) for shift_by in (grid_cols, -grid_cols)
    ]
    window = jnp.stack([column_parts[0], row_strip, column_parts[1]])
    key_tiles = window[:, :, 0].reshape(9 * frames, tile_len, feature_width)
    value_tiles = window[:, :, 1].reshape(9 * frames, tile_len, feature_width)
    kept_mask = tile_mask == 1
    first_offset = 9
    slot_count = 9
    slot_order = jnp.arange(first_offset, first_offset + slot_count, dtype=jnp.int32)[None, :]
    slot_kept = kept_mask[:, first_offset : first_offset + slot_count]
    frame_ids = jnp.arange(frames, dtype=jnp.int32)[:, None]
    source_frame = jnp.clip(frame_ids + slot_order // 9 - 1, 0, frames - 1)
    source = slot_order % 9 * frames + source_frame
    kept_cols = jnp.repeat(slot_kept, tile_len, axis=1)[:, None, :]
    score_scale = 1.0 / math.sqrt(HDIM)

    def one_head(head_index):
        column_start = head_index * HDIM
        key_head = lax.dynamic_slice_in_dim(key_tiles, column_start, HDIM, 2)
        value_head = lax.dynamic_slice_in_dim(value_tiles, column_start, HDIM, 2)
        query_head = lax.dynamic_slice_in_dim(query_local, column_start, HDIM, 1).reshape(
            frames, tile_len, HDIM
        )
        picked_keys = jnp.take(key_head, source, axis=0).reshape(
            frames, slot_count * tile_len, HDIM
        )
        picked_values = jnp.take(value_head, source, axis=0).reshape(
            frames, slot_count * tile_len, HDIM
        )
        scores = (
            jnp.einsum("fqd,fkd->fqk", query_head, picked_keys, preferred_element_type=jnp.float32)
            * score_scale
        )
        row_peak = jnp.max(jnp.where(kept_cols, scores, -jnp.inf), axis=2, keepdims=True)
        weight = jnp.exp(jnp.where(kept_cols, scores - row_peak, -jnp.inf))
        row_total = jnp.sum(weight, axis=2, keepdims=True)
        rounded = weight.astype(jnp.bfloat16)
        mixed = jnp.einsum(
            "fqk,fkd->fqd", rounded, picked_values, preferred_element_type=jnp.float32
        )
        return (mixed / row_total).astype(jnp.bfloat16)

    result = lax.map(one_head, jnp.arange(head_count, dtype=jnp.int32))
    result = jnp.transpose(result, (1, 2, 0, 3)).reshape(frames * tile_len, feature_width)
    return lax.all_to_all(result, "head", split_axis=0, concat_axis=1, tiled=True)


AXES = ("pair", "mate", "head")
AHEAD = (1, 3, 0, 2)
BEHIND = (2, 0, 3, 1)
ACROSS = (3, 2, 1, 0)
MASKED = -1e30
FACTOR = math.log2(math.e) / math.sqrt(HDIM)


def flipped(index, bits, size):
    out, step = 0, 1
    while step < size:
        bit = (index // step) % 2
        out = out + step * (1 - bit if (bits // step) % 2 else bit)
        step *= 2
    return out


def columns_of(mate, l, heads, width):
    group = mate * heads + flipped(lax.axis_index("head"), l, heads)
    return pl.ds(pl.multiple_of(group * width, 128), width)


def copy_all(copies, sem):
    copies = [pltpu.make_async_copy(a, b, sem.at[n]) for n, (a, b) in enumerate(copies)]
    for copy in copies:
        copy.start()
    for copy in copies:
        copy.wait()


def cut_ahead_kernel(heads, width, k_ref, v_ref, *rest):
    outs, sem = rest[:-1], rest[-1]
    copies = []
    for l, out in enumerate(outs):
        cols = columns_of(1 - lax.axis_index("pair"), l, heads, width)
        for n, part in enumerate((k_ref, v_ref)):
            copies.append((part.at[:, cols], out.at[:, n * width : (n + 1) * width]))
    copy_all(copies, sem)


def cut_rest_kernel(heads, width, q_ref, k_ref, v_ref, *rest):
    outs, sem = rest[:-1], rest[-1]
    own = lax.axis_index("mate")
    mates = (own, 1 - own, lax.axis_index("pair"))
    copies = []
    for i, out in enumerate(outs[: 3 * heads]):
        cols = columns_of(mates[i // heads], i % heads, heads, width)
        for n, part in enumerate((k_ref, v_ref)):
            copies.append((part.at[:, cols], out.at[:, n * width : (n + 1) * width]))
    for s, out in enumerate(outs[3 * heads :]):
        cols = columns_of(mates[s // heads], s % heads, heads, width)
        copies.append((q_ref.at[:, cols], out))
    copy_all(copies, sem)


def cut_call(kernel, inputs, key_values, queries, heads, width):
    rows = inputs[0].shape[0]
    shapes = [jax.ShapeDtypeStruct((rows, 2 * width), jnp.bfloat16)] * key_values
    shapes += [jax.ShapeDtypeStruct((rows, width), jnp.bfloat16)] * queries
    return pl.pallas_call(
        functools.partial(kernel, heads, width),
        out_shape=shapes,
        in_specs=[pl.BlockSpec(memory_space=pltpu.VMEM)] * len(inputs),
        out_specs=[pl.BlockSpec(memory_space=pl.ANY)] * len(shapes),
        scratch_shapes=[pltpu.SemaphoreType.DMA((2 * key_values + queries,))],
    )(*inputs)


def tile_bias(masks, own, key_blocks, tile):
    z = lax.axis_index("pair") * 2 + lax.axis_index("mate")

    def place(block):
        p = (block + 3) % 4
        return p // 2, p % 2

    row, col = place(flipped(z, own, 4))
    lane_tile = lax.broadcasted_iota(jnp.int32, (1, len(key_blocks) * tile), 1) // tile
    bias = jnp.zeros(lane_tile.shape, jnp.float32)
    for n, block in enumerate(key_blocks):
        key_row, key_col = place(block)
        offset = 9 + 3 * (key_row - row + 1) + (key_col - col + 1)
        dropped = masks[own][0, offset] != 1
        bias = jnp.where((lane_tile == n) & dropped, MASKED, bias)
    return bias


def key_blocks():
    pair, mate = lax.axis_index("pair"), lax.axis_index("mate")
    z = 2 * pair + mate
    return z, 2 * (1 - mate) + pair, 3 - z, 2 * mate + 1 - pair


def softmax_part(q, k, v, bias):
    scores = lax.dot_general(q, k, (((1,), (1,)), ((), ())), preferred_element_type=jnp.float32)
    scores = scores + bias
    peak = jnp.max(scores, axis=1, keepdims=True)
    weight = jnp.exp2((scores - peak) * FACTOR)
    total = jnp.sum(weight, axis=1, keepdims=True)
    mixed = jnp.dot(weight.astype(jnp.bfloat16), v, preferred_element_type=jnp.float32)
    return peak, total, mixed


def first_kernel(heads, width, *refs):
    masks, refs = refs[:2], refs[2:]
    queries, refs = refs[: 2 * heads], refs[2 * heads :]
    pieces, refs = refs[: 3 * heads], refs[3 * heads :]
    q_out, stat_out, mixed_out, kbuf, vbuf = refs
    rows = queries[0].shape[0]
    tile = heads * rows
    for s, piece in enumerate(queries):
        q_out[s * rows : (s + 1) * rows, :] = piece[...]
    for s, piece in enumerate(pieces):
        kbuf[s * rows : (s + 1) * rows, :] = piece[:, :width]
        vbuf[s * rows : (s + 1) * rows, :] = piece[:, width:]
    for own in range(2):
        bias = tile_bias(masks, own, key_blocks()[:3], tile)
        at = slice(own * tile, (own + 1) * tile)
        for h in range(width // HDIM):
            cols = slice(h * HDIM, (h + 1) * HDIM)
            peak, total, mixed = softmax_part(q_out[at, cols], kbuf[:, cols], vbuf[:, cols], bias)
            stat_out[at, 2 * h : 2 * h + 1] = peak
            stat_out[at, 2 * h + 1 : 2 * h + 2] = total
            mixed_out[at, cols] = mixed


def last_kernel(heads, width, *refs):
    masks, refs = refs[:2], refs[2:]
    q_ref, stat_ref, mixed_ref, refs = refs[0], refs[1], refs[2], refs[3:]
    pieces, refs = refs[:heads], refs[heads:]
    outs, kbuf, vbuf = refs[: 2 * heads], refs[2 * heads], refs[2 * heads + 1]
    rows = pieces[0].shape[0]
    tile = heads * rows
    for s, piece in enumerate(pieces):
        kbuf[s * rows : (s + 1) * rows, :] = piece[:, :width]
        vbuf[s * rows : (s + 1) * rows, :] = piece[:, width:]
    for own in range(2):
        bias = tile_bias(masks, own, key_blocks()[3:], tile)
        at = slice(own * tile, (own + 1) * tile)
        for h in range(width // HDIM):
            cols = slice(h * HDIM, (h + 1) * HDIM)
            peak, total, mixed = softmax_part(q_ref[at, cols], kbuf[:, cols], vbuf[:, cols], bias)
            old_peak = stat_ref[at, 2 * h : 2 * h + 1]
            old_total = stat_ref[at, 2 * h + 1 : 2 * h + 2]
            top = jnp.maximum(peak, old_peak)
            new_share = jnp.exp2((peak - top) * FACTOR)
            old_share = jnp.exp2((old_peak - top) * FACTOR)
            total = total * new_share + old_total * old_share
            mixed = mixed * new_share + mixed_ref[at, cols] * old_share
            result = (mixed / total).astype(jnp.bfloat16)
            for n in range(heads):
                outs[own * heads + n][:, cols] = result[n * rows : (n + 1) * rows]


def attend_first(masks, queries, pieces, heads, width):
    rows = pieces[0].shape[0]
    tile = heads * rows
    vmem = pl.BlockSpec(memory_space=pltpu.VMEM)
    return pl.pallas_call(
        functools.partial(first_kernel, heads, width),
        out_shape=[
            jax.ShapeDtypeStruct((2 * tile, width), jnp.bfloat16),
            jax.ShapeDtypeStruct((2 * tile, 128), jnp.float32),
            jax.ShapeDtypeStruct((2 * tile, width), jnp.float32),
        ],
        in_specs=[pl.BlockSpec(memory_space=pltpu.SMEM)] * 2
        + [vmem] * (len(queries) + len(pieces)),
        out_specs=[vmem] * 3,
        scratch_shapes=[pltpu.VMEM((3 * tile, width), jnp.bfloat16)] * 2,
        name="first",
    )(*masks, *queries, *pieces)


def attend_last(masks, carried, pieces, heads, width):
    rows = pieces[0].shape[0]
    tile = heads * rows
    vmem = pl.BlockSpec(memory_space=pltpu.VMEM)
    return pl.pallas_call(
        functools.partial(last_kernel, heads, width),
        out_shape=[jax.ShapeDtypeStruct((rows, width), jnp.bfloat16)] * (2 * heads),
        in_specs=[pl.BlockSpec(memory_space=pltpu.SMEM)] * 2 + [vmem] * (3 + len(pieces)),
        out_specs=[vmem] * (2 * heads),
        scratch_shapes=[pltpu.VMEM((tile, width), jnp.bfloat16)] * 2,
        name="last",
    )(*masks, *carried, *pieces)


def join_kernel(heads, width, *refs):
    pieces, out = refs[:-1], refs[-1]
    own = lax.axis_index("mate")
    for s, piece in enumerate(pieces):
        mate = 1 - own if s >= heads else own
        out[:, columns_of(mate, s % heads, heads, width)] = piece[...]


def join(pieces, heads, width):
    rows = pieces[0].shape[0]
    vmem = pl.BlockSpec(memory_space=pltpu.VMEM)
    return pl.pallas_call(
        functools.partial(join_kernel, heads, width),
        out_shape=jax.ShapeDtypeStruct((rows, 2 * heads * width), jnp.bfloat16),
        in_specs=[vmem] * len(pieces),
        out_specs=vmem,
        name="join",
    )(*pieces)


def moved(block, pattern, l, heads):
    route = [
        (z * heads + h, pattern[z] * heads + (h ^ l)) for z in range(4) for h in range(heads)
    ]
    return lax.ppermute(block, AXES, route)


OWN, MATE = (0, 1, 2, 3), (1, 0, 3, 2)


def on_device_square(query_rows, key_rows, value_rows, tile_mask):
    heads = lax.axis_size("head")
    width = query_rows.shape[1] // (2 * heads)
    some = range(heads)
    sent = cut_call(cut_ahead_kernel, (key_rows, value_rows), heads, 0, heads, width)
    ahead = [moved(sent[l], AHEAD, l, heads) for l in some]
    inputs = (query_rows, key_rows, value_rows)
    rest = cut_call(cut_rest_kernel, inputs, 3 * heads, 2 * heads, heads, width)
    asked = rest[3 * heads :]
    queries = [asked[0]] + [
        moved(asked[s], MATE if s >= heads else OWN, s % heads, heads)
        for s in range(1, 2 * heads)
    ]
    own = [rest[0]] + [moved(rest[l], OWN, l, heads) for l in some[1:]]
    across = [moved(rest[heads + l], ACROSS, l, heads) for l in some]
    behind = [moved(rest[2 * heads + l], BEHIND, l, heads) for l in some]
    masks = (tile_mask, moved(tile_mask, MATE, 0, heads))
    carried = attend_first(masks, queries, own + ahead + across, heads, width)
    parts = attend_last(masks, carried, behind, heads, width)
    order = [s for s in range(heads, 2 * heads)] + list(some[1:])
    back = {0: parts[0]}
    for s in order:
        back[s] = moved(parts[s], MATE if s >= heads else OWN, s % heads, heads)
    return join([back[s] for s in range(2 * heads)], heads, width)


def solution(mesh):
    groups, ctx, heads = (mesh.shape[name] for name in ("groups", "ctx", "head"))
    if ctx == 4 and heads & (heads - 1) == 0:
        square = Mesh(mesh.devices.reshape(groups, 2, 2, heads), ("groups",) + AXES)
        rows = P(("groups",) + AXES, None)
        return jax.shard_map(
            on_device_square,
            mesh=square,
            in_specs=(rows, rows, rows, P(("groups", "pair", "mate"), None)),
            out_specs=rows,
            check_vma=False,
        )
    rows = P(("groups", "ctx", "head"), None)
    return jax.shard_map(
        on_device,
        mesh=mesh,
        in_specs=(rows, rows, rows, P(("groups", "ctx"), None)),
        out_specs=rows,
        check_vma=False,
    )
```

```python
import functools
import math

import jax
import jax.numpy as jnp
from jax import lax
from jax.experimental import pallas as pl
from jax.experimental.pallas import tpu as pltpu
from jax.sharding import Mesh, PartitionSpec as P


HDIM = 128


def passed_along(block, axis, distance):
    devices = range(lax.axis_size(axis))
    route = [((i - distance) % len(devices), i) for i in devices]
    return lax.ppermute(block, axis, route)


def on_device(query_rows, key_rows, value_rows, tile_mask):
    cycle_size = lax.axis_size("ctx")
    grid_rows = max(2, cycle_size // 8)
    grid_cols = cycle_size // grid_rows
    query_local, key_local, value_local = (
        lax.all_to_all(query_rows, "head", split_axis=1, concat_axis=0, tiled=True),
        lax.all_to_all(key_rows, "head", split_axis=1, concat_axis=0, tiled=True),
        lax.all_to_all(value_rows, "head", split_axis=1, concat_axis=0, tiled=True),
    )
    feature_width = query_local.shape[1]
    head_count = feature_width // HDIM
    frames = tile_mask.shape[0]
    tile_len = query_local.shape[0] // frames
    key_value = jnp.stack([key_local, value_local]).reshape(2, frames, tile_len, feature_width)
    row_parts = [passed_along(key_value, "ctx", shift_by) for shift_by in (1, -1)]
    row_strip = jnp.stack([row_parts[0], key_value, row_parts[1]])
    column_parts = [
        passed_along(row_strip, "ctx", shift_by) for shift_by in (grid_cols, -grid_cols)
    ]
    window = jnp.stack([column_parts[0], row_strip, column_parts[1]])
    key_tiles = window[:, :, 0].reshape(9 * frames, tile_len, feature_width)
    value_tiles = window[:, :, 1].reshape(9 * frames, tile_len, feature_width)
    kept_mask = tile_mask == 1
    first_offset = 9
    slot_count = 9
    slot_order = jnp.arange(first_offset, first_offset + slot_count, dtype=jnp.int32)[None, :]
    slot_kept = kept_mask[:, first_offset : first_offset + slot_count]
    frame_ids = jnp.arange(frames, dtype=jnp.int32)[:, None]
    source_frame = jnp.clip(frame_ids + slot_order // 9 - 1, 0, frames - 1)
    source = slot_order % 9 * frames + source_frame
    kept_cols = jnp.repeat(slot_kept, tile_len, axis=1)[:, None, :]
    score_scale = 1.0 / math.sqrt(HDIM)

    def one_head(head_index):
        column_start = head_index * HDIM
        key_head = lax.dynamic_slice_in_dim(key_tiles, column_start, HDIM, 2)
        value_head = lax.dynamic_slice_in_dim(value_tiles, column_start, HDIM, 2)
        query_head = lax.dynamic_slice_in_dim(query_local, column_start, HDIM, 1).reshape(
            frames, tile_len, HDIM
        )
        picked_keys = jnp.take(key_head, source, axis=0).reshape(
            frames, slot_count * tile_len, HDIM
        )
        picked_values = jnp.take(value_head, source, axis=0).reshape(
            frames, slot_count * tile_len, HDIM
        )
        scores = (
            jnp.einsum("fqd,fkd->fqk", query_head, picked_keys, preferred_element_type=jnp.float32)
            * score_scale
        )
        row_peak = jnp.max(jnp.where(kept_cols, scores, -jnp.inf), axis=2, keepdims=True)
        weight = jnp.exp(jnp.where(kept_cols, scores - row_peak, -jnp.inf))
        row_total = jnp.sum(weight, axis=2, keepdims=True)
        rounded = weight.astype(jnp.bfloat16)
        mixed = jnp.einsum(
            "fqk,fkd->fqd", rounded, picked_values, preferred_element_type=jnp.float32
        )
        return (mixed / row_total).astype(jnp.bfloat16)

    result = lax.map(one_head, jnp.arange(head_count, dtype=jnp.int32))
    result = jnp.transpose(result, (1, 2, 0, 3)).reshape(frames * tile_len, feature_width)
    return lax.all_to_all(result, "head", split_axis=0, concat_axis=1, tiled=True)


AXES = ("pair", "mate", "head")
AHEAD = (1, 3, 0, 2)
BEHIND = (2, 0, 3, 1)
ACROSS = (3, 2, 1, 0)
MASKED = -1e30
FACTOR = math.log2(math.e) / math.sqrt(HDIM)
KERNEL_VMEM = 28 << 20


def flipped(index, bits, size):
    out, step = 0, 1
    while step < size:
        bit = (index // step) % 2
        out = out + step * (1 - bit if (bits // step) % 2 else bit)
        step *= 2
    return out


def columns_of(mate, l, heads, width):
    group = mate * heads + flipped(lax.axis_index("head"), l, heads)
    return pl.ds(pl.multiple_of(group * width, 128), width)


def copy_all(copies, sem):
    copies = [pltpu.make_async_copy(a, b, sem.at[n]) for n, (a, b) in enumerate(copies)]
    for copy in copies:
        copy.start()
    for copy in copies:
        copy.wait()


def cut_ahead_kernel(heads, width, k_ref, v_ref, *rest):
    outs, sem = rest[:-1], rest[-1]
    copies = []
    for l, out in enumerate(outs):
        cols = columns_of(1 - lax.axis_index("pair"), l, heads, width)
        for n, part in enumerate((k_ref, v_ref)):
            copies.append((part.at[:, cols], out.at[:, n * width : (n + 1) * width]))
    copy_all(copies, sem)


def cut_rest_kernel(heads, width, q_ref, k_ref, v_ref, *rest):
    outs, sem = rest[:-1], rest[-1]
    own = lax.axis_index("mate")
    mates = (own, 1 - own, lax.axis_index("pair"))
    copies = []
    for i, out in enumerate(outs[: 3 * heads]):
        cols = columns_of(mates[i // heads], i % heads, heads, width)
        for n, part in enumerate((k_ref, v_ref)):
            copies.append((part.at[:, cols], out.at[:, n * width : (n + 1) * width]))
    for s, out in enumerate(outs[3 * heads :]):
        cols = columns_of(mates[s // heads], s % heads, heads, width)
        copies.append((q_ref.at[:, cols], out))
    copy_all(copies, sem)


def cut_call(kernel, inputs, key_values, queries, heads, width):
    rows = inputs[0].shape[0]
    shapes = [jax.ShapeDtypeStruct((rows, 2 * width), jnp.bfloat16)] * key_values
    shapes += [jax.ShapeDtypeStruct((rows, width), jnp.bfloat16)] * queries
    return pl.pallas_call(
        functools.partial(kernel, heads, width),
        out_shape=shapes,
        in_specs=[pl.BlockSpec(memory_space=pltpu.VMEM)] * len(inputs),
        out_specs=[pl.BlockSpec(memory_space=pl.ANY)] * len(shapes),
        scratch_shapes=[pltpu.SemaphoreType.DMA((2 * key_values + queries,))],
    )(*inputs)


def tile_bias(masks, own, key_blocks, tile):
    z = lax.axis_index("pair") * 2 + lax.axis_index("mate")

    def place(block):
        p = (block + 3) % 4
        return p // 2, p % 2

    row, col = place(flipped(z, own, 4))
    lane_tile = lax.broadcasted_iota(jnp.int32, (1, len(key_blocks) * tile), 1) // tile
    bias = jnp.zeros(lane_tile.shape, jnp.float32)
    for n, block in enumerate(key_blocks):
        key_row, key_col = place(block)
        offset = 9 + 3 * (key_row - row + 1) + (key_col - col + 1)
        dropped = masks[own][0, offset] != 1
        bias = jnp.where((lane_tile == n) & dropped, MASKED, bias)
    return bias


def key_blocks():
    pair, mate = lax.axis_index("pair"), lax.axis_index("mate")
    z = 2 * pair + mate
    return z, 2 * (1 - mate) + pair, 3 - z, 2 * mate + 1 - pair


def fill(kbuf, vbuf, pieces, width):
    rows = pieces[0].shape[0]
    ones = jnp.ones((rows, HDIM), jnp.bfloat16)
    for s, piece in enumerate(pieces):
        at = slice(s * rows, (s + 1) * rows)
        kbuf[at, :] = piece[:, :width]
        for h in range(width // HDIM):
            vbuf[at, 2 * h * HDIM : (2 * h + 1) * HDIM] = piece[
                :, width + h * HDIM : width + (h + 1) * HDIM
            ]
            vbuf[at, (2 * h + 1) * HDIM : (2 * h + 2) * HDIM] = ones


def scores_of(q, k, bias):
    scores = lax.dot_general(q, k, (((1,), (1,)), ((), ())), preferred_element_type=jnp.float32)
    return scores + bias


def mixed_of(scores, peak, v):
    weight = jnp.exp2((scores - peak) * FACTOR).astype(jnp.bfloat16)
    return jnp.dot(weight, v, preferred_element_type=jnp.float32)


def first_kernel(heads, width, *refs):
    masks, refs = refs[:2], refs[2:]
    queries, refs = refs[: 2 * heads], refs[2 * heads :]
    pieces, refs = refs[: 2 * heads], refs[2 * heads :]
    q_out, peak_out, mixed_out, kbuf, vbuf = refs
    rows = queries[0].shape[0]
    tile = heads * rows
    for s, piece in enumerate(queries):
        q_out[s * rows : (s + 1) * rows, :] = piece[...]
    fill(kbuf, vbuf, pieces, width)
    for own in range(2):
        bias = tile_bias(masks, own, key_blocks()[:2], tile)
        at = slice(own * tile, (own + 1) * tile)
        for h in range(width // HDIM):
            cols = slice(h * HDIM, (h + 1) * HDIM)
            both = slice(2 * h * HDIM, (2 * h + 2) * HDIM)
            scores = scores_of(q_out[at, cols], kbuf[:, cols], bias)
            peak = jnp.max(scores, axis=1, keepdims=True)
            peak_out[at, cols] = jnp.broadcast_to(peak, (tile, HDIM))
            mixed_out[at, both] = mixed_of(scores, peak, vbuf[:, both])


def last_kernel(heads, width, *refs):
    masks, refs = refs[:2], refs[2:]
    q_ref, peak_ref, mixed_ref, refs = refs[0], refs[1], refs[2], refs[3:]
    pieces, refs = refs[: 2 * heads], refs[2 * heads :]
    outs, kbuf, vbuf = refs[: 2 * heads], refs[2 * heads], refs[2 * heads + 1]
    rows = pieces[0].shape[0]
    tile = heads * rows
    fill(kbuf, vbuf, pieces, width)
    for own in (1, 0):
        bias = tile_bias(masks, own, key_blocks()[2:], tile)
        at = slice(own * tile, (own + 1) * tile)
        for h in range(width // HDIM):
            cols = slice(h * HDIM, (h + 1) * HDIM)
            both = slice(2 * h * HDIM, (2 * h + 2) * HDIM)
            scores = scores_of(q_ref[at, cols], kbuf[:, cols], bias)
            old_peak = peak_ref[at, cols]
            peak = jnp.broadcast_to(jnp.max(scores, axis=1, keepdims=True), (tile, HDIM))
            peak = jnp.maximum(peak, old_peak)
            share = jnp.exp2((old_peak - peak) * FACTOR)
            wide = jnp.concatenate([peak] * (2 * tile // HDIM), axis=1)
            mixed = mixed_of(scores, wide, vbuf[:, both])
            total = mixed[:, HDIM:] + mixed_ref[at, both][:, HDIM:] * share
            mixed = mixed[:, :HDIM] + mixed_ref[at, both][:, :HDIM] * share
            result = (mixed / total).astype(jnp.bfloat16)
            for n in range(heads):
                outs[own * heads + n][:, cols] = result[n * rows : (n + 1) * rows]


def attend_first(masks, queries, pieces, heads, width):
    rows = pieces[0].shape[0]
    tile = heads * rows
    vmem = pl.BlockSpec(memory_space=pltpu.VMEM)
    return pl.pallas_call(
        functools.partial(first_kernel, heads, width),
        out_shape=[
            jax.ShapeDtypeStruct((2 * tile, width), jnp.bfloat16),
            jax.ShapeDtypeStruct((2 * tile, width), jnp.float32),
            jax.ShapeDtypeStruct((2 * tile, 2 * width), jnp.float32),
        ],
        in_specs=[pl.BlockSpec(memory_space=pltpu.SMEM)] * 2
        + [vmem] * (len(queries) + len(pieces)),
        out_specs=[vmem] * 3,
        scratch_shapes=[
            pltpu.VMEM((2 * tile, width), jnp.bfloat16),
            pltpu.VMEM((2 * tile, 2 * width), jnp.bfloat16),
        ],
        compiler_params=pltpu.CompilerParams(vmem_limit_bytes=KERNEL_VMEM),
        name="first",
    )(*masks, *queries, *pieces)


def attend_last(masks, carried, pieces, heads, width):
    rows = pieces[0].shape[0]
    tile = heads * rows
    vmem = pl.BlockSpec(memory_space=pltpu.VMEM)
    return pl.pallas_call(
        functools.partial(last_kernel, heads, width),
        out_shape=[jax.ShapeDtypeStruct((rows, width), jnp.bfloat16)] * (2 * heads),
        in_specs=[pl.BlockSpec(memory_space=pltpu.SMEM)] * 2 + [vmem] * (3 + len(pieces)),
        out_specs=[vmem] * (2 * heads),
        scratch_shapes=[
            pltpu.VMEM((2 * tile, width), jnp.bfloat16),
            pltpu.VMEM((2 * tile, 2 * width), jnp.bfloat16),
        ],
        compiler_params=pltpu.CompilerParams(vmem_limit_bytes=KERNEL_VMEM),
        name="last",
    )(*masks, *carried, *pieces)


def join_kernel(heads, width, *refs):
    pieces, out, sem = refs[:-2], refs[-2], refs[-1]
    own = lax.axis_index("mate")
    copies = []
    for s, piece in enumerate(pieces):
        mate = 1 - own if s >= heads else own
        copies.append((piece, out.at[:, columns_of(mate, s % heads, heads, width)]))
    copy_all(copies, sem)


def join(pieces, heads, width):
    rows = pieces[0].shape[0]
    return pl.pallas_call(
        functools.partial(join_kernel, heads, width),
        out_shape=jax.ShapeDtypeStruct((rows, 2 * heads * width), jnp.bfloat16),
        in_specs=[pl.BlockSpec(memory_space=pltpu.VMEM)] * len(pieces),
        out_specs=pl.BlockSpec(memory_space=pl.ANY),
        scratch_shapes=[pltpu.SemaphoreType.DMA((len(pieces),))],
        name="join",
    )(*pieces)


def moved(block, pattern, l, heads):
    route = [
        (z * heads + h, pattern[z] * heads + (h ^ l)) for z in range(4) for h in range(heads)
    ]
    return lax.ppermute(block, AXES, route)


OWN, MATE = (0, 1, 2, 3), (1, 0, 3, 2)


def on_device_square(query_rows, key_rows, value_rows, tile_mask):
    heads = lax.axis_size("head")
    width = query_rows.shape[1] // (2 * heads)
    some = range(heads)
    sent = cut_call(cut_ahead_kernel, (key_rows, value_rows), heads, 0, heads, width)
    ahead = [moved(sent[l], AHEAD, l, heads) for l in some]
    inputs = (query_rows, key_rows, value_rows)
    rest = cut_call(cut_rest_kernel, inputs, 3 * heads, 2 * heads, heads, width)
    asked = rest[3 * heads :]
    queries = [asked[0]] + [
        moved(asked[s], MATE if s >= heads else OWN, s % heads, heads)
        for s in range(1, 2 * heads)
    ]
    own = [rest[0]] + [moved(rest[l], OWN, l, heads) for l in some[1:]]
    across = [moved(rest[heads + l], ACROSS, l, heads) for l in some]
    behind = [moved(rest[2 * heads + l], BEHIND, l, heads) for l in some]
    masks = (tile_mask, moved(tile_mask, MATE, 0, heads))
    carried = attend_first(masks, queries, own + ahead, heads, width)
    parts = attend_last(masks, carried, across + behind, heads, width)
    order = [s for s in range(heads, 2 * heads)] + list(some[1:])
    back = {0: parts[0]}
    for s in order:
        back[s] = moved(parts[s], MATE if s >= heads else OWN, s % heads, heads)
    return join([back[s] for s in range(2 * heads)], heads, width)


def solution(mesh):
    groups, ctx, heads = (mesh.shape[name] for name in ("groups", "ctx", "head"))
    if ctx == 4 and heads & (heads - 1) == 0:
        square = Mesh(mesh.devices.reshape(groups, 2, 2, heads), ("groups",) + AXES)
        rows = P(("groups",) + AXES, None)
        return jax.shard_map(
            on_device_square,
            mesh=square,
            in_specs=(rows, rows, rows, P(("groups", "pair", "mate"), None)),
            out_specs=rows,
            check_vma=False,
        )
    rows = P(("groups", "ctx", "head"), None)
    return jax.shard_map(
        on_device,
        mesh=mesh,
        in_specs=(rows, rows, rows, P(("groups", "ctx"), None)),
        out_specs=rows,
        check_vma=False,
    )
```
